512 devices in a mesh: samp: 64 (over z, y), trait: 8 (over x, core).
Axes of the slice: x: 4, y: 8, z: 8, core: 2. Of those that a mesh axis runs over, the one named last changes fastest.
Arguments:
- samples: bfloat16 [32768, 2048], P('samp'), may hold values from -18 to 18
- traits: bfloat16 [32768, 2048], P('samp', 'trait'), may hold values from -6 to 6
- whitening: bfloat16 [2048, 2048], P(None, 'trait'), may hold values from -0.0017089844 to 0.0017089844
- singular: float32 [2048], replicated, may hold values from 0.3 to 3
- lambdas: float32 [4], replicated, may hold values from 0.1 to 10
Outputs:
- loo_residual: float32 [4, 32768, 2048], P(None, 'samp', 'trait')
The draws below stay inside these ranges and needn't reach their ends.
All inputs are finite; a program needn't handle non-finite values.
Results may differ from the reference program's by a relative error of at most 0.0041.
Values may be sent and summed in bfloat16 or wider, within the bound.
No kernel may reach another device: no remote copies, remote signals or barrier semaphores. Data moves between devices by JAX's collectives and lax.ppermute only.
A program may use at most 64 MiB of HBM per device.

```python
import math
import jax
import jax.numpy as jnp
from jax import lax

P_SIZE = 2048
T_SIZE = 2048
NL = 4
SAMPLES = 32768


def draw_samples(key, part):
    first_key, second_key = jax.random.split(jax.random.fold_in(key, 11), 2)
    row_scale = jnp.exp(jax.random.uniform(first_key, (SAMPLES, 1), jnp.float32, jnp.log(0.3), jnp.log(3.0)))
    base_values = jnp.clip(jax.random.normal(second_key, (SAMPLES, P_SIZE), jnp.float32), -6.0, 6.0)
    return (base_values * row_scale).astype(jnp.bfloat16)


def block_levels(stream_key, dims, cuts, low, top_value):
    def one(axis_at, shards_of):
        draws = jax.random.uniform(jax.random.fold_in(jax.random.fold_in(stream_key, 6), axis_at), (shards_of,), jnp.float32, low / len(cuts), top_value / len(cuts))
        return jnp.repeat(jnp.exp(draws), dims[axis_at] // shards_of).reshape((-1,) + (1,) * (len(dims) - axis_at - 1))

    gain = one(*cuts[0])
    for cut in cuts[1:]:
        gain = gain * one(*cut)
    return gain


def normal_values(stream_key, shape, scale, reach, cuts=(), kind=jnp.bfloat16):
    array = scale * jax.random.normal(stream_key, shape, jnp.float32)
    if cuts:
        array = array * block_levels(stream_key, shape, cuts, -0.22, 0.18)
    return jnp.clip(array, -reach, reach).astype(kind)


def setup_inputs(seed: int = 0) -> dict:
    seeds = jax.random.split(jax.random.key(seed), 6)
    samples = draw_samples(jax.random.fold_in(seeds[5], 71), 0)
    traits = normal_values(seeds[1], (SAMPLES, T_SIZE), 1.0, 6.0, ((0, 64), (1, 8)))
    whitening = normal_values(seeds[2], (P_SIZE, P_SIZE), (10 * P_SIZE * P_SIZE // 3) ** -0.5, 0.0017089844, ((1, 8),))
    singular = jnp.clip(jnp.exp(jax.random.uniform(seeds[3], (P_SIZE,), jnp.float32, math.log(0.3), math.log(3.0))), 0.3, 3.0)
    lambdas = jnp.clip(jnp.exp(jax.random.uniform(seeds[4], (NL,), jnp.float32, math.log(0.1), math.log(10.0))), 0.1, 10.0)
    return {"samples": samples, "traits": traits, "whitening": whitening, "singular": singular, "lambdas": lambdas}


def reference(samples, traits, whitening, singular, lambdas):
    components = jnp.dot(samples, whitening, preferred_element_type=jnp.float32).astype(jnp.bfloat16)
    squared_values = singular * singular
    shrink = squared_values[:, None] / (squared_values[:, None] + lambdas[None, :])
    wide_float = components.astype(jnp.float32)
    leverage = jnp.dot(wide_float * wide_float, shrink, precision=lax.Precision.HIGHEST)
    projected = jnp.dot(components.T, traits, preferred_element_type=jnp.float32).astype(jnp.bfloat16)
    target = traits.astype(jnp.float32)
    results = []
    for penalty in range(NL):
        scaled = (shrink[:, penalty:penalty + 1] * projected.astype(jnp.float32)).astype(jnp.bfloat16)
        fitted = jnp.dot(components, scaled, preferred_element_type=jnp.float32)
        divisor = jnp.maximum(1.0 - leverage[:, penalty:penalty + 1], 0.25)
        results.append((target - fitted) / divisor)
    return jnp.stack(results, axis=0)
```

```python
import jax
import jax.numpy as jnp
from jax import lax
from jax.sharding import Mesh, PartitionSpec as P

SAMP = ("z", "y")
TRAIT = ("x", "core")


def local(samples, traits, whitening, singular, lambdas):
    depth = whitening.shape[1]
    rows = samples.shape[0]
    width = traits.shape[1]
    n_x, n_core = lax.axis_size("x"), lax.axis_size("core")
    n_samp = lax.axis_size("z") * lax.axis_size("y")
    core = lax.axis_index("core")

    own = jnp.dot(samples, whitening, preferred_element_type=jnp.float32).astype(jnp.bfloat16)
    mine = lax.all_to_all(jnp.broadcast_to(own[None], (n_x, rows, depth)), "x", 0, 0)
    other = lax.ppermute(mine, "core", [(0, 1), (1, 0)])
    halves = [
        jnp.moveaxis(half, 0, 1).reshape(rows, n_x * depth) for half in (mine, other)
    ]

    squared = (singular * singular).reshape(n_x, n_core, depth)
    squared = jnp.moveaxis(squared, 1, 0).reshape(n_core, n_x * depth)
    squared = jnp.where(core == 0, squared, squared[::-1])
    shrink = squared[None] / (squared[None] + lambdas[:, None, None])

    flipped = traits.T
    partial = jnp.stack(
        [jnp.dot(flipped, half, preferred_element_type=jnp.float32) for half in halves]
    ).astype(jnp.bfloat16)
    pieces = partial.reshape(n_samp, -1, n_x * depth)
    arrived = lax.all_to_all(pieces, SAMP, 0, 0)
    total = jnp.sum(arrived.astype(jnp.float32), axis=0).astype(jnp.bfloat16)
    spread = lax.all_to_all(jnp.broadcast_to(total[None], pieces.shape), SAMP, 0, 0)
    projected = spread.reshape(n_core, width, n_x * depth)

    leverage = 0.0
    fitted = 0.0
    for i, half in enumerate(halves):
        wide = half.astype(jnp.float32)
        leverage = leverage + jnp.dot(
            shrink[:, i], (wide * wide).T, precision=lax.Precision.HIGHEST
        )
        scaled = (shrink[:, i, None, :] * projected[i].astype(jnp.float32)[None]).astype(jnp.bfloat16)
        fitted = fitted + jnp.einsum("np,ltp->lnt", half, scaled, preferred_element_type=jnp.float32)
    divisor = jnp.maximum(1.0 - leverage[:, :, None], 0.25)
    return (traits.astype(jnp.float32)[None] - fitted) / divisor


def solution(mesh):
    split = Mesh(mesh.devices.reshape(8, 8, 4, 2), SAMP + TRAIT)
    return jax.shard_map(
        local,
        mesh=split,
        in_specs=(P(SAMP, None), P(SAMP, TRAIT), P(None, TRAIT), P(), P()),
        out_specs=P(None, SAMP, TRAIT),
        check_vma=False,
    )
```

```python
import jax
import jax.numpy as jnp
from jax import lax
from jax.experimental import pallas as pl
from jax.experimental.pallas import tpu as pltpu
from jax.sharding import Mesh, PartitionSpec as P

SAMP = ("z", "y")
TRAIT = ("x", "core")
MIB = 1 << 20


def whole(*shape):
    return pl.BlockSpec(shape, lambda *_: (0,) * len(shape))


def call(body, out, grid, in_specs, out_specs, flops, moved, vmem, scratch=()):
    return pl.pallas_call(
        body,
        out_shape=out,
        grid=grid,
        in_specs=in_specs,
        out_specs=out_specs,
        scratch_shapes=list(scratch),
        compiler_params=pltpu.CompilerParams(vmem_limit_bytes=vmem * MIB),
        cost_estimate=pl.CostEstimate(flops=flops, bytes_accessed=moved, transcendentals=0),
    )


def own_body(samples, whitening, out):
    block = jnp.dot(samples[...], whitening[...], preferred_element_type=jnp.float32)
    out[...] = jnp.broadcast_to(block.astype(jnp.bfloat16)[None], out.shape)


def partial_body(traits, mine, other, out):
    flipped = traits[...].T
    n_x, _, depth = mine.shape
    groups = out.shape[0] // 2
    for half, source in enumerate((mine, other)):
        for j in range(n_x):
            piece = jnp.dot(flipped, source[j], preferred_element_type=jnp.float32)
            out[half * groups : (half + 1) * groups, :, j * depth : (j + 1) * depth] = (
                piece.astype(jnp.bfloat16).reshape(groups, -1, depth)
            )


def sum_body(arrived, out):
    total = arrived[0].astype(jnp.float32)
    for i in range(1, arrived.shape[0]):
        total = total + arrived[i].astype(jnp.float32)
    total = total.astype(jnp.bfloat16)
    for i in range(out.shape[0]):
        out[i] = total


def leverage_body(core, lambdas, squared, mine, other, joined, inverse):
    n_x, rows, depth = mine.shape
    n_l = inverse.shape[0]
    step = 128
    sums = [jnp.zeros((rows, step), jnp.float32) for _ in range(n_l)]
    for half, source in enumerate((mine, other)):
        line = squared[pl.ds(lax.rem(core[0] + half, 2), 1), :]
        for j in range(n_x):
            for at in range(0, depth, step):
                here = j * depth + at
                value = source[j, :, at : at + step]
                start = half * n_x * depth + here
                joined[:, start : start + step] = value
                wide = value.astype(jnp.float32)
                wide = wide * wide
                top = line[:, here : here + step]
                for l in range(n_l):
                    sums[l] = sums[l] + wide * (top / (top + lambdas[l]))
    for l in range(n_l):
        level = jnp.sum(sums[l], axis=1, keepdims=True)
        inverse[l] = 1.0 / jnp.maximum(1.0 - level, 0.25)


def fitted_body(core, lambdas, squared, joined, projected, traits, inverse, out, scaled):
    l = pl.program_id(0)
    groups = projected.shape[0] // 2
    span = projected.shape[2]
    for half in range(2):
        top = squared[pl.ds(lax.rem(core[0] + half, 2), 1), :]
        shrink = top / (top + lambdas[l])
        values = projected[half * groups : (half + 1) * groups].reshape(-1, span)
        scaled[:, half * span : (half + 1) * span] = (
            values.astype(jnp.float32) * shrink
        ).astype(jnp.bfloat16)
    fitted = lax.dot_general(
        joined[...], scaled[...], (((1,), (1,)), ((), ())), preferred_element_type=jnp.float32
    )
    out[0] = (traits[...].astype(jnp.float32) - fitted) * inverse[0]


def local(samples, traits, whitening, singular, lambdas):
    features, depth = whitening.shape
    rows, width = traits.shape
    n_x, n_core = lax.axis_size("x"), lax.axis_size("core")
    n_samp = lax.axis_size("z") * lax.axis_size("y")
    n_l = lambdas.shape[0]
    span = n_x * depth
    every = n_core * span
    bf16, f32 = jnp.bfloat16, jnp.float32
    core = lax.axis_index("core").astype(jnp.int32).reshape(1)
    squared = jnp.moveaxis((singular * singular).reshape(n_x, n_core, depth), 1, 0)
    squared = squared.reshape(n_core, span)
    scalar = pl.BlockSpec(memory_space=pltpu.SMEM)

    block = 128
    own = call(
        own_body,
        jax.ShapeDtypeStruct((n_x, rows, depth), bf16),
        (rows // block,),
        [pl.BlockSpec((block, features), lambda i: (i, 0)), whole(features, depth)],
        pl.BlockSpec((n_x, block, depth), lambda i: (0, i, 0)),
        2 * rows * features * depth,
        2 * (rows * features + features * depth + n_x * rows * depth),
        12,
    )(samples, whitening)
    mine = lax.all_to_all(own, "x", 0, 0)
    other = lax.ppermute(mine, "core", [(0, 1), (1, 0)])

    pieces = (n_samp, n_core * width // n_samp, span)
    partial = call(
        partial_body,
        jax.ShapeDtypeStruct(pieces, bf16),
        (1,),
        [whole(rows, width), whole(n_x, rows, depth), whole(n_x, rows, depth)],
        whole(*pieces),
        2 * rows * width * every,
        2 * (rows * width + rows * every + every * width),
        16,
    )(traits, mine, other)
    arrived = lax.all_to_all(partial, SAMP, 0, 0)
    total = call(
        sum_body,
        jax.ShapeDtypeStruct(pieces, bf16),
        (1,),
        [whole(*pieces)],
        whole(*pieces),
        every * width,
        4 * every * width,
        8,
    )(arrived)
    projected = lax.all_to_all(total, SAMP, 0, 0)

    joined, inverse = call(
        leverage_body,
        (
            jax.ShapeDtypeStruct((rows, every), bf16),
            jax.ShapeDtypeStruct((n_l, rows, 1), f32),
        ),
        (rows // block,),
        [
            scalar,
            scalar,
            whole(n_core, span),
            pl.BlockSpec((n_x, block, depth), lambda i: (0, i, 0)),
            pl.BlockSpec((n_x, block, depth), lambda i: (0, i, 0)),
        ],
        (
            pl.BlockSpec((block, every), lambda i: (i, 0)),
            pl.BlockSpec((n_l, block, 1), lambda i: (0, i, 0)),
        ),
        10 * rows * every,
        4 * rows * every,
        16,
    )(core, lambdas, squared, mine, other)
    return call(
        fitted_body,
        jax.ShapeDtypeStruct((n_l, rows, width), f32),
        (n_l,),
        [
            scalar,
            scalar,
            whole(n_core, span),
            whole(rows, every),
            whole(*pieces),
            whole(rows, width),
            pl.BlockSpec((1, rows, 1), lambda l: (l, 0, 0)),
        ],
        pl.BlockSpec((1, rows, width), lambda l: (l, 0, 0)),
        2 * n_l * rows * every * width,
        2 * rows * every + 2 * every * width + 4 * n_l * rows * width,
        16,
        [pltpu.VMEM((width, every), bf16)],
    )(core, lambdas, squared, joined, projected, traits, inverse)


def solution(mesh):
    split = Mesh(mesh.devices.reshape(8, 8, 4, 2), SAMP + TRAIT)
    return jax.shard_map(
        local,
        mesh=split,
        in_specs=(P(SAMP, None), P(SAMP, TRAIT), P(None, TRAIT), P(), P()),
        out_specs=P(None, SAMP, TRAIT),
        check_vma=False,
    )
```

```python
import jax
import jax.numpy as jnp
from jax import lax
from jax.experimental import pallas as pl
from jax.experimental.pallas import tpu as pltpu
from jax.sharding import Mesh, PartitionSpec as P


SAMP = ("z", "y")
TRAIT = ("x", "core")
FULL = 67043328
SMALL = 8 << 20
EARLY = ((0, 0), (0, 1), (1, 0), (3, 0))
LATE = ((1, 1), (3, 1), (2, 0), (2, 1))
HBM = pl.BlockSpec(memory_space=pltpu.HBM)
SCALAR = pl.BlockSpec(memory_space=pltpu.SMEM)


def whole(*shape):
    return pl.BlockSpec(shape, lambda *_: (0,) * len(shape))


def call(body, out, in_specs, out_specs, flops, moved, vmem, scratch=(), grid=(1,)):
    return pl.pallas_call(
        body,
        out_shape=out,
        grid=grid,
        in_specs=in_specs,
        out_specs=out_specs,
        scratch_shapes=list(scratch),
        compiler_params=pltpu.CompilerParams(vmem_limit_bytes=vmem),
        cost_estimate=pl.CostEstimate(flops=flops, bytes_accessed=moved, transcendentals=0),
    )


def cross_body(samples, traits, out, samples_v, traits_v, sems):
    n = samples_v.shape[0]
    _, cols = samples_v.shape[1:]
    copies = [pltpu.make_async_copy(traits, traits_v, sems.at[n])]
    for i in range(n):
        copies.append(
            pltpu.make_async_copy(
                samples.at[:, i * cols : (i + 1) * cols], samples_v.at[i], sems.at[i]
            )
        )
    for copy in copies:
        copy.start()
    copies[0].wait()
    flipped = traits_v[...].T
    span = out.shape[2]
    groups = out.shape[0] // 2
    for i in range(n):
        copies[i + 1].wait()
        piece = jnp.dot(flipped, samples_v[i], preferred_element_type=jnp.float32)
        half, at = divmod(i * cols, span)
        out[half * groups : (half + 1) * groups, :, at : at + cols] = piece.astype(
            jnp.bfloat16
        ).reshape(groups, -1, cols)


def sum_body(arrived, out):
    total = arrived[0].astype(jnp.float32)
    for i in range(1, arrived.shape[0]):
        total = total + arrived[i].astype(jnp.float32)
    total = total.astype(jnp.bfloat16)
    for i in range(out.shape[0]):
        out[i] = total


def row_of(place, shift, swap):
    return lax.rem(place[0] + 4 - shift, 4) * 2 + lax.rem(place[1] + swap, 2)


def components_body(first, order, *refs):
    n = len(order)
    place, lambdas, squared, samples = refs[:4]
    blocks = refs[4 : 4 + n]
    before = () if first else (refs[4 + n],)
    out, level, samples_v, blocks_v, sems = refs[-5:]
    copies = [pltpu.make_async_copy(samples, samples_v, sems.at[n])]
    for i in range(n):
        copies.append(pltpu.make_async_copy(blocks[i], blocks_v.at[i], sems.at[i]))
    for copy in copies:
        copy.start()
    copies[0].wait()
    rows, depth = samples_v.shape[0], blocks_v.shape[2]
    n_l = level.shape[0]
    step = 128
    sums = [jnp.zeros((rows, step), jnp.float32) for _ in range(n_l)]
    for i, (shift, swap) in enumerate(order):
        copies[i + 1].wait()
        value = jnp.dot(samples_v[...], blocks_v[i], preferred_element_type=jnp.float32)
        value = value.astype(jnp.bfloat16)
        out[:, i * depth : (i + 1) * depth] = value
        wide = value.astype(jnp.float32)
        wide = wide * wide
        top = squared[pl.ds(row_of(place, shift, swap), 1), :]
        for l in range(n_l):
            shrink = top / (top + lambdas[l])
            for at in range(0, depth, step):
                sums[l] = sums[l] + wide[:, at : at + step] * shrink[:, at : at + step]
    for l in range(n_l):
        total = jnp.sum(sums[l], axis=1, keepdims=True)
        if first:
            level[l] = total
        else:
            level[l] = 1.0 / jnp.maximum(1.0 - (before[0][l] + total), 0.25)


def fitted_body(order, *refs):
    n = len(order)
    place, lambdas, squared, inverse, early, late, cross, traits = refs[:8]
    blocks = refs[8 : 8 + n]
    out, cross_v, early_v, late_v, traits_v, blocks_v, projected, scaled, sems = refs[-9:]
    l = pl.program_id(0)
    depth = blocks_v.shape[2]
    span = cross_v.shape[2]
    groups = cross_v.shape[0] // 2

    @pl.when(l == 0)
    def _():
        pairs = [(cross, cross_v)]
        pairs += [(blocks[i], blocks_v.at[i]) for i in range(n)]
        pairs += [(early, early_v), (late, late_v), (traits, traits_v)]
        copies = [
            pltpu.make_async_copy(source, target, sems.at[i])
            for i, (source, target) in enumerate(pairs)
        ]
        for copy in copies:
            copy.start()
        copies[0].wait()
        for i in range(n):
            copies[i + 1].wait()
            value = 0.0
            for half in range(2):
                value = value + jnp.dot(
                    cross_v[half * groups : (half + 1) * groups].reshape(-1, span),
                    blocks_v[i, half * span : (half + 1) * span, :],
                    preferred_element_type=jnp.float32,
                )
            projected[:, i * depth : (i + 1) * depth] = value.astype(jnp.bfloat16)
        for copy in copies[n + 1 :]:
            copy.wait()

    for i, (shift, swap) in enumerate(order):
        top = squared[pl.ds(row_of(place, shift, swap), 1), :]
        shrink = top / (top + lambdas[l])
        here = slice(i * depth, (i + 1) * depth)
        scaled[:, here] = (projected[:, here].astype(jnp.float32) * shrink).astype(jnp.bfloat16)
    contract = (((1,), (1,)), ((), ()))
    middle = early_v.shape[1]
    fitted = lax.dot_general(
        early_v[...], scaled[:, :middle], contract, preferred_element_type=jnp.float32
    ) + lax.dot_general(
        late_v[...], scaled[:, middle:], contract, preferred_element_type=jnp.float32
    )
    out[0] = (traits_v[...].astype(jnp.float32) - fitted) * inverse[0]


def compute(samples, traits, whitening, singular, lambdas):
    features, depth = whitening.shape
    rows, width = traits.shape
    n_x, n_core = lax.axis_size("x"), lax.axis_size("core")
    n_samp = lax.axis_size("z") * lax.axis_size("y")
    n_l = lambdas.shape[0]
    every = n_x * n_core * depth
    n_blocks = n_x * n_core
    bf16, f32 = jnp.bfloat16, jnp.float32
    place = jnp.stack([lax.axis_index("x"), lax.axis_index("core")]).astype(jnp.int32)
    squared = (singular * singular).reshape(n_blocks, depth)
    dma = pltpu.SemaphoreType.DMA

    pieces = (n_samp, 2 * width // n_samp, features // 2)
    partial = call(
        cross_body,
        jax.ShapeDtypeStruct(pieces, bf16),
        [HBM, HBM],
        whole(*pieces),
        2 * rows * width * features,
        2 * (rows * width + rows * features + features * width),
        FULL,
        [
            pltpu.VMEM((8, rows, features // 8), bf16),
            pltpu.VMEM((rows, width), bf16),
            dma((9,)),
        ],
    )(samples, traits)
    arrived = lax.all_to_all(partial, SAMP, 0, 0)

    shifts = {}
    for shift in (1, 3, 2):
        shifts[shift] = lax.ppermute(
            whitening, "x", [(i, (i + shift) % n_x) for i in range(n_x)]
        )
    blocks = {(0, 0): whitening}
    for shift in (0, 1, 3, 2):
        if shift:
            blocks[shift, 0] = shifts[shift]
        blocks[shift, 1] = lax.ppermute(blocks[shift, 0], "core", [(0, 1), (1, 0)])

    total = call(
        sum_body,
        jax.ShapeDtypeStruct(pieces, bf16),
        [whole(*pieces)],
        whole(*pieces),
        features * width,
        4 * features * width,
        SMALL,
    )(arrived)
    cross = lax.all_to_all(total, SAMP, 0, 0)

    def components(order, first, extra):
        n = len(order)
        return call(
            lambda *refs: components_body(first, order, *refs),
            (
                jax.ShapeDtypeStruct((rows, n * depth), bf16),
                jax.ShapeDtypeStruct((n_l, rows, 1), f32),
            ),
            [SCALAR, SCALAR, whole(n_blocks, depth)]
            + [HBM] * (n + 1)
            + [whole(n_l, rows, 1)] * (not first),
            (whole(rows, n * depth), whole(n_l, rows, 1)),
            2 * rows * features * n * depth,
            2 * (rows * features + features * n * depth + rows * n * depth),
            FULL,
            [
                pltpu.VMEM((rows, features), bf16),
                pltpu.VMEM((n, features, depth), bf16),
                dma((n + 1,)),
            ],
        )(place, lambdas, squared, samples, *[blocks[b] for b in order], *extra)

    early, level = components(EARLY, True, ())
    late, inverse = components(LATE, False, (level,))

    order = EARLY + LATE
    return call(
        lambda *refs: fitted_body(order, *refs),
        jax.ShapeDtypeStruct((n_l, rows, width), f32),
        [
            SCALAR,
            SCALAR,
            whole(n_blocks, depth),
            pl.BlockSpec((1, rows, 1), lambda l: (l, 0, 0)),
        ]
        + [HBM] * (n_blocks + 4),
        pl.BlockSpec((1, rows, width), lambda l: (l, 0, 0)),
        2 * n_l * rows * every * width,
        2 * rows * every + 2 * every * width + 4 * n_l * rows * width,
        FULL,
        [
            pltpu.VMEM(pieces, bf16),
            pltpu.VMEM((rows, every // 2), bf16),
            pltpu.VMEM((rows, every // 2), bf16),
            pltpu.VMEM((rows, width), bf16),
            pltpu.VMEM((n_blocks, features, depth), bf16),
            pltpu.VMEM((width, every), bf16),
            pltpu.VMEM((width, every), bf16),
            dma((n_blocks + 4,)),
        ],
        grid=(n_l,),
    )(
        place, lambdas, squared, inverse, early, late, cross, traits,
        *[blocks[b] for b in order],
    )


def solution(mesh):
    split = Mesh(mesh.devices.reshape(8, 8, 4, 2), SAMP + TRAIT)
    return jax.shard_map(
        compute,
        mesh=split,
        in_specs=(P(SAMP, None), P(SAMP, TRAIT), P(None, TRAIT), P(), P()),
        out_specs=P(None, SAMP, TRAIT),
        check_vma=False,
    )
```

```python
import jax
import jax.numpy as jnp
from jax import lax
from jax.experimental import pallas as pl
from jax.experimental.pallas import tpu as pltpu
from jax.sharding import Mesh, PartitionSpec as P


SAMP = ("z", "y")
TRAIT = ("x", "core")
FULL = 67043328
SMALL = 8 << 20
GROUPS = (((0, 0), (0, 1)), ((2, 0), (2, 1)), ((1, 0), (3, 0), (1, 1), (3, 1)))
HBM = pl.BlockSpec(memory_space=pltpu.HBM)
SCALAR = pl.BlockSpec(memory_space=pltpu.SMEM)


def whole(*shape):
    return pl.BlockSpec(shape, lambda *_: (0,) * len(shape))


def call(body, out, in_specs, out_specs, flops, moved, vmem, scratch=(), grid=(1,)):
    return pl.pallas_call(
        body,
        out_shape=out,
        grid=grid,
        in_specs=in_specs,
        out_specs=out_specs,
        scratch_shapes=list(scratch),
        compiler_params=pltpu.CompilerParams(vmem_limit_bytes=vmem),
        cost_estimate=pl.CostEstimate(flops=flops, bytes_accessed=moved, transcendentals=0),
    )


def cross_body(samples, traits, out, samples_v, traits_v, sems):
    n = samples_v.shape[0]
    _, cols = samples_v.shape[1:]
    copies = [pltpu.make_async_copy(traits, traits_v, sems.at[n])]
    for i in range(n):
        copies.append(
            pltpu.make_async_copy(
                samples.at[:, i * cols : (i + 1) * cols], samples_v.at[i], sems.at[i]
            )
        )
    for copy in copies:
        copy.start()
    copies[0].wait()
    flipped = traits_v[...].T
    span = out.shape[2]
    groups = out.shape[0] // 2
    for i in range(n):
        copies[i + 1].wait()
        piece = jnp.dot(flipped, samples_v[i], preferred_element_type=jnp.float32)
        half, at = divmod(i * cols, span)
        out[half * groups : (half + 1) * groups, :, at : at + cols] = piece.astype(
            jnp.bfloat16
        ).reshape(groups, -1, cols)


def sum_body(arrived, out):
    total = arrived[0].astype(jnp.float32)
    for i in range(1, arrived.shape[0]):
        total = total + arrived[i].astype(jnp.float32)
    total = total.astype(jnp.bfloat16)
    for i in range(out.shape[0]):
        out[i] = total


def row_of(place, shift, swap):
    return lax.rem(place[0] + 4 - shift, 4) * 2 + lax.rem(place[1] + swap, 2)


def split(value):
    top = value.astype(jnp.bfloat16)
    return top, value - top.astype(jnp.float32)


def shrink_of(place, squared, lambdas, block, penalties):
    top = squared[pl.ds(row_of(place, *block), 1), :]
    return [top / (top + lambdas[l]) for l in penalties]


def components_body(first, last, order, *refs):
    n = len(order)
    place, lambdas, squared, samples = refs[:4]
    blocks = refs[4 : 4 + n]
    out, level, samples_v, blocks_v, sems = refs[-5:]
    copies = [pltpu.make_async_copy(samples, samples_v, sems.at[n])]
    for i in range(n):
        copies.append(pltpu.make_async_copy(blocks[i], blocks_v.at[i], sems.at[i]))
    for copy in copies:
        copy.start()
    depth = blocks_v.shape[2]
    n_l = lambdas.shape[0]
    total = jnp.zeros((samples_v.shape[0], 2 * n_l), jnp.float32) if first else refs[4 + n][...]
    copies[0].wait()
    for i, block in enumerate(order):
        copies[i + 1].wait()
        value = jnp.dot(samples_v[...], blocks_v[i], preferred_element_type=jnp.float32)
        value = value.astype(jnp.bfloat16)
        out[:, i * depth : (i + 1) * depth] = value
        wide = value.astype(jnp.float32)
        high, low = split(wide * wide)
        shrink = jnp.concatenate(shrink_of(place, squared, lambdas, block, range(n_l)), axis=0)
        coarse, fine = split(shrink)
        weight = jnp.concatenate([coarse.astype(jnp.float32), fine], axis=0).astype(jnp.bfloat16)
        for part in (high, low.astype(jnp.bfloat16)):
            total = total + lax.dot_general(
                part, weight, (((1,), (1,)), ((), ())), preferred_element_type=jnp.float32
            )
    if last:
        level[...] = 1.0 / jnp.maximum(1.0 - (total[:, :n_l] + total[:, n_l:]), 0.25)
    else:
        level[...] = total


def fitted_body(groups_of, order, *refs):
    n, n_groups = len(order), len(groups_of)
    place, lambdas, squared, inverse, cross, traits = refs[:6]
    parts = refs[6 : 6 + n_groups]
    blocks = refs[6 + n_groups : 6 + n_groups + n]
    out, cross_v, joined, traits_v, blocks_v, projected, scaled, out_v, sems, out_sems = refs[-10:]
    depth = blocks_v.shape[2]
    span = cross_v.shape[2]
    half_groups = cross_v.shape[0] // 2
    pairs = [(cross, cross_v)]
    pairs += [(blocks[i], blocks_v.at[i]) for i in range(n)]
    at = 0
    for part in parts:
        pairs.append((part, joined.at[:, at : at + part.shape[1]]))
        at += part.shape[1]
    pairs.append((traits, traits_v))
    copies = [
        pltpu.make_async_copy(source, target, sems.at[i])
        for i, (source, target) in enumerate(pairs)
    ]
    for copy in copies:
        copy.start()
    copies[0].wait()
    halves = [
        cross_v[half * half_groups : (half + 1) * half_groups].reshape(-1, span)
        for half in range(2)
    ]
    for i in range(n):
        copies[i + 1].wait()
        value = 0.0
        for half in range(2):
            value = value + jnp.dot(
                halves[half],
                blocks_v[i, half * span : (half + 1) * span, :],
                preferred_element_type=jnp.float32,
            )
        projected[:, i * depth : (i + 1) * depth] = value.astype(jnp.bfloat16)
    for copy in copies[n + 1 :]:
        copy.wait()
    n_l = lambdas.shape[0]
    results = []
    for l in range(n_l):
        for i, block in enumerate(order):
            (shrink,) = shrink_of(place, squared, lambdas, block, (l,))
            here = slice(i * depth, (i + 1) * depth)
            scaled[l % 2, :, here] = (projected[:, here].astype(jnp.float32) * shrink).astype(
                jnp.bfloat16
            )
        fitted = lax.dot_general(
            joined[...],
            scaled[l % 2],
            (((1,), (1,)), ((), ())),
            preferred_element_type=jnp.float32,
        )
        out_v[l] = (traits_v[...].astype(jnp.float32) - fitted) * inverse[:, l : l + 1]
        results.append(pltpu.make_async_copy(out_v.at[l], out.at[l], out_sems.at[l]))
        results[-1].start()
    for copy in results:
        copy.wait()


def compute(samples, traits, whitening, singular, lambdas):
    features, depth = whitening.shape
    rows, width = traits.shape
    n_x, n_core = lax.axis_size("x"), lax.axis_size("core")
    n_samp = lax.axis_size("z") * lax.axis_size("y")
    n_l = lambdas.shape[0]
    every = n_x * n_core * depth
    n_blocks = n_x * n_core
    bf16, f32 = jnp.bfloat16, jnp.float32
    place = jnp.stack([lax.axis_index("x"), lax.axis_index("core")]).astype(jnp.int32)
    squared = (singular * singular).reshape(n_blocks, depth)
    dma = pltpu.SemaphoreType.DMA

    pieces = (n_samp, 2 * width // n_samp, features // 2)
    partial = call(
        cross_body,
        jax.ShapeDtypeStruct(pieces, bf16),
        [HBM, HBM],
        whole(*pieces),
        2 * rows * width * features,
        2 * (rows * width + rows * features + features * width),
        FULL,
        [pltpu.VMEM((8, rows, features // 8), bf16), pltpu.VMEM((rows, width), bf16), dma((9,))],
    )(samples, traits)
    arrived = lax.all_to_all(partial, SAMP, 0, 0)

    shifts = {}
    for shift in (2, 1, 3):
        shifts[shift] = lax.ppermute(whitening, "x", [(i, (i + shift) % n_x) for i in range(n_x)])
    blocks = {(0, 0): whitening}
    for shift in (0, 2, 1, 3):
        if shift:
            blocks[shift, 0] = shifts[shift]
        blocks[shift, 1] = lax.ppermute(blocks[shift, 0], "core", [(0, 1), (1, 0)])

    total = call(
        sum_body,
        jax.ShapeDtypeStruct(pieces, bf16),
        [whole(*pieces)],
        whole(*pieces),
        features * width,
        4 * features * width,
        SMALL,
    )(arrived)
    cross = lax.all_to_all(total, SAMP, 0, 0)

    def components(order, extra, last):
        n = len(order)
        first = not extra
        columns = n_l if last else 2 * n_l
        return call(
            lambda *refs: components_body(first, last, order, *refs),
            (
                jax.ShapeDtypeStruct((rows, n * depth), bf16),
                jax.ShapeDtypeStruct((rows, columns), f32),
            ),
            [SCALAR, SCALAR, whole(n_blocks, depth)]
            + [HBM] * (n + 1)
            + [whole(rows, 2 * n_l)] * len(extra),
            (whole(rows, n * depth), whole(rows, columns)),
            2 * rows * features * n * depth,
            2 * (rows * features + features * n * depth + rows * n * depth),
            FULL,
            [
                pltpu.VMEM((rows, features), bf16),
                pltpu.VMEM((n, features, depth), bf16),
                dma((n + 1,)),
            ],
        )(place, lambdas, squared, samples, *[blocks[b] for b in order], *extra)

    parts, state = [], ()
    for i, group in enumerate(GROUPS):
        part, level = components(group, state, i == len(GROUPS) - 1)
        parts.append(part)
        state = (level,)

    order = sum(GROUPS, ())
    return call(
        lambda *refs: fitted_body(GROUPS, order, *refs),
        jax.ShapeDtypeStruct((n_l, rows, width), f32),
        [SCALAR, SCALAR, whole(n_blocks, depth), whole(rows, n_l)]
        + [HBM] * (n_blocks + len(GROUPS) + 2),
        HBM,
        2 * n_l * rows * every * width,
        2 * rows * every + 2 * every * width + 4 * n_l * rows * width,
        FULL,
        [
            pltpu.VMEM(pieces, bf16),
            pltpu.VMEM((rows, every), bf16),
            pltpu.VMEM((rows, width), bf16),
            pltpu.VMEM((n_blocks, features, depth), bf16),
            pltpu.VMEM((width, every), bf16),
            pltpu.VMEM((2, width, every), bf16),
            pltpu.VMEM((n_l, rows, width), f32),
            dma((n_blocks + len(GROUPS) + 2,)),
            dma((n_l,)),
        ],
    )(
        place, lambdas, squared, level, cross, traits,
        *parts,
        *[blocks[b] for b in order],
    )


def solution(mesh):
    split = Mesh(mesh.devices.reshape(8, 8, 4, 2), SAMP + TRAIT)
    return jax.shard_map(
        compute,
        mesh=split,
        in_specs=(P(SAMP, None), P(SAMP, TRAIT), P(None, TRAIT), P(), P()),
        out_specs=P(None, SAMP, TRAIT),
        check_vma=False,
    )
```

```python
import jax
import jax.numpy as jnp
from jax import lax
from jax.experimental import pallas as pl
from jax.experimental.pallas import tpu as pltpu
from jax.sharding import Mesh, PartitionSpec as P


SAMP = ("z", "y")
TRAIT = ("x", "core")
FULL = 67043328
SMALL = 8 << 20
GROUPS = (((0, 0), (0, 1)), ((1, 0), (3, 0), (1, 1), (3, 1)), ((2, 0), (2, 1)))
HBM = pl.BlockSpec(memory_space=pltpu.HBM)
SCALAR = pl.BlockSpec(memory_space=pltpu.SMEM)


def whole(*shape):
    return pl.BlockSpec(shape, lambda *_: (0,) * len(shape))


def call(body, out, in_specs, out_specs, flops, moved, vmem, scratch=(), grid=(1,)):
    return pl.pallas_call(
        body,
        out_shape=out,
        grid=grid,
        in_specs=in_specs,
        out_specs=out_specs,
        scratch_shapes=list(scratch),
        compiler_params=pltpu.CompilerParams(vmem_limit_bytes=vmem),
        cost_estimate=pl.CostEstimate(flops=flops, bytes_accessed=moved, transcendentals=0),
    )


def cross_body(samples, traits, out, samples_v, traits_v, sems):
    n = samples_v.shape[0]
    _, cols = samples_v.shape[1:]
    copies = [pltpu.make_async_copy(traits, traits_v, sems.at[n])]
    for i in range(n):
        copies.append(
            pltpu.make_async_copy(
                samples.at[:, i * cols : (i + 1) * cols], samples_v.at[i], sems.at[i]
            )
        )
    for copy in copies:
        copy.start()
    copies[0].wait()
    flipped = traits_v[...].T
    span = out.shape[2]
    groups = out.shape[0] // 2
    for i in range(n):
        copies[i + 1].wait()
        piece = jnp.dot(flipped, samples_v[i], preferred_element_type=jnp.float32)
        half, at = divmod(i * cols, span)
        out[half * groups : (half + 1) * groups, :, at : at + cols] = piece.astype(
            jnp.bfloat16
        ).reshape(groups, -1, cols)


def sum_body(arrived, out):
    total = arrived[0].astype(jnp.float32)
    for i in range(1, arrived.shape[0]):
        total = total + arrived[i].astype(jnp.float32)
    total = total.astype(jnp.bfloat16)
    for i in range(out.shape[0]):
        out[i] = total


def row_of(place, shift, swap):
    return lax.rem(place[0] + 4 - shift, 4) * 2 + lax.rem(place[1] + swap, 2)


def split(value):
    top = value.astype(jnp.bfloat16)
    return top, value - top.astype(jnp.float32)


def shrink_of(place, squared, lambdas, block, penalties):
    top = squared[pl.ds(row_of(place, *block), 1), :]
    return [top / (top + lambdas[l]) for l in penalties]


def components_body(first, last, order, *refs):
    n = len(order)
    place, lambdas, squared, samples = refs[:4]
    blocks = refs[4 : 4 + n]
    out, level, samples_v, blocks_v, sems = refs[-5:]
    depth = blocks[0].shape[1]
    n_l = lambdas.shape[0]
    copies = [pltpu.make_async_copy(samples, samples_v, sems.at[n])]
    for i in range(n):
        copies.append(
            pltpu.make_async_copy(
                blocks[i], blocks_v.at[:, i * depth : (i + 1) * depth], sems.at[i]
            )
        )
    for copy in copies:
        copy.start()
    total = jnp.zeros((samples_v.shape[0], 2 * n_l), jnp.float32) if first else refs[4 + n][...]
    copies[0].wait()
    for i in range(0, n, 2):
        copies[i + 1].wait()
        copies[i + 2].wait()
        here = slice(i * depth, (i + 2) * depth)
        value = jnp.dot(
            samples_v[...], blocks_v[:, here], preferred_element_type=jnp.float32
        ).astype(jnp.bfloat16)
        out[:, here] = value
        wide = value.astype(jnp.float32)
        high, low = split(wide * wide)
        shrink = jnp.concatenate(
            [
                jnp.concatenate(shrink_of(place, squared, lambdas, block, range(n_l)), axis=0)
                for block in order[i : i + 2]
            ],
            axis=1,
        )
        coarse, fine = split(shrink)
        weight = jnp.concatenate([coarse.astype(jnp.float32), fine], axis=0).astype(jnp.bfloat16)
        for part in (high, low.astype(jnp.bfloat16)):
            total = total + lax.dot_general(
                part, weight, (((1,), (1,)), ((), ())), preferred_element_type=jnp.float32
            )
    if last:
        level[...] = 1.0 / jnp.maximum(1.0 - (total[:, :n_l] + total[:, n_l:]), 0.25)
    else:
        level[...] = total


def fitted_body(groups_of, order, *refs):
    n, n_groups = len(order), len(groups_of)
    place, lambdas, squared, inverse, cross, traits = refs[:6]
    parts = refs[6 : 6 + n_groups]
    blocks = refs[6 + n_groups : 6 + n_groups + n]
    out, cross_v, joined, traits_v, blocks_v, projected, scaled, out_v, sems, out_sems = refs[-10:]
    depth = blocks[0].shape[1]
    width, span = cross.shape[1:]
    pairs = [(cross.at[half], cross_v.at[:, half * span : (half + 1) * span]) for half in range(2)]
    pairs += [(blocks[i], blocks_v.at[:, i * depth : (i + 1) * depth]) for i in range(n)]
    at = 0
    for part in parts:
        pairs.append((part, joined.at[:, at : at + part.shape[1]]))
        at += part.shape[1]
    pairs.append((traits, traits_v))
    copies = [
        pltpu.make_async_copy(source, target, sems.at[i])
        for i, (source, target) in enumerate(pairs)
    ]
    for copy in copies:
        copy.start()
    copies[0].wait()
    copies[1].wait()
    for i in range(0, n, 2):
        copies[i + 2].wait()
        copies[i + 3].wait()
        here = slice(i * depth, (i + 2) * depth)
        projected[:, here] = jnp.dot(
            cross_v[...], blocks_v[:, here], preferred_element_type=jnp.float32
        ).astype(jnp.bfloat16)
    for copy in copies[n + 2 :]:
        copy.wait()
    n_l = lambdas.shape[0]
    results = []
    for pair in range(n_l // 2):
        for i, block in enumerate(order):
            here = slice(i * depth, (i + 1) * depth)
            value = projected[:, here].astype(jnp.float32)
            for j, shrink in enumerate(
                shrink_of(place, squared, lambdas, block, (2 * pair, 2 * pair + 1))
            ):
                scaled[pair, j * width : (j + 1) * width, here] = (value * shrink).astype(
                    jnp.bfloat16
                )
        fitted = lax.dot_general(
            joined[...],
            scaled[pair],
            (((1,), (1,)), ((), ())),
            preferred_element_type=jnp.float32,
        )
        for j in range(2):
            l = 2 * pair + j
            out_v[l] = (
                traits_v[...].astype(jnp.float32) - fitted[:, j * width : (j + 1) * width]
            ) * inverse[:, l : l + 1]
            results.append(pltpu.make_async_copy(out_v.at[l], out.at[l], out_sems.at[l]))
            results[-1].start()
    for copy in results:
        copy.wait()


def compute(samples, traits, whitening, singular, lambdas):
    features, depth = whitening.shape
    rows, width = traits.shape
    n_x, n_core = lax.axis_size("x"), lax.axis_size("core")
    n_samp = lax.axis_size("z") * lax.axis_size("y")
    n_l = lambdas.shape[0]
    every = n_x * n_core * depth
    n_blocks = n_x * n_core
    bf16, f32 = jnp.bfloat16, jnp.float32
    place = jnp.stack([lax.axis_index("x"), lax.axis_index("core")]).astype(jnp.int32)
    squared = (singular * singular).reshape(n_blocks, depth)
    dma = pltpu.SemaphoreType.DMA

    pieces = (n_samp, 2 * width // n_samp, features // 2)
    partial = call(
        cross_body,
        jax.ShapeDtypeStruct(pieces, bf16),
        [HBM, HBM],
        whole(*pieces),
        2 * rows * width * features,
        2 * (rows * width + rows * features + features * width),
        FULL,
        [pltpu.VMEM((8, rows, features // 8), bf16), pltpu.VMEM((rows, width), bf16), dma((9,))],
    )(samples, traits)
    arrived = lax.all_to_all(partial, SAMP, 0, 0)

    shifts = {}
    for shift in (2, 1, 3):
        shifts[shift] = lax.ppermute(whitening, "x", [(i, (i + shift) % n_x) for i in range(n_x)])
    blocks = {(0, 0): whitening}
    for shift in (0, 2, 1, 3):
        if shift:
            blocks[shift, 0] = shifts[shift]
        blocks[shift, 1] = lax.ppermute(blocks[shift, 0], "core", [(0, 1), (1, 0)])

    total = call(
        sum_body,
        jax.ShapeDtypeStruct(pieces, bf16),
        [whole(*pieces)],
        whole(*pieces),
        features * width,
        4 * features * width,
        SMALL,
    )(arrived)
    cross = lax.all_to_all(total, SAMP, 0, 0)

    def components(order, extra, last):
        n = len(order)
        first = not extra
        columns = n_l if last else 2 * n_l
        return call(
            lambda *refs: components_body(first, last, order, *refs),
            (
                jax.ShapeDtypeStruct((rows, n * depth), bf16),
                jax.ShapeDtypeStruct((rows, columns), f32),
            ),
            [SCALAR, SCALAR, whole(n_blocks, depth)]
            + [HBM] * (n + 1)
            + [whole(rows, 2 * n_l)] * len(extra),
            (whole(rows, n * depth), whole(rows, columns)),
            2 * rows * features * n * depth,
            2 * (rows * features + features * n * depth + rows * n * depth),
            FULL,
            [
                pltpu.VMEM((rows, features), bf16),
                pltpu.VMEM((features, n * depth), bf16),
                dma((n + 1,)),
            ],
        )(place, lambdas, squared, samples, *[blocks[b] for b in order], *extra)

    parts, state = [], ()
    for i, group in enumerate(GROUPS):
        part, level = components(group, state, i == len(GROUPS) - 1)
        parts.append(part)
        state = (level,)

    order = sum(GROUPS, ())
    return call(
        lambda *refs: fitted_body(GROUPS, order, *refs),
        jax.ShapeDtypeStruct((n_l, rows, width), f32),
        [SCALAR, SCALAR, whole(n_blocks, depth), whole(rows, n_l)]
        + [HBM] * (n_blocks + len(GROUPS) + 2),
        HBM,
        2 * n_l * rows * every * width,
        2 * rows * every + 2 * every * width + 4 * n_l * rows * width,
        FULL,
        [
            pltpu.VMEM((width, features), bf16),
            pltpu.VMEM((rows, every), bf16),
            pltpu.VMEM((rows, width), bf16),
            pltpu.VMEM((features, every), bf16),
            pltpu.VMEM((width, every), bf16),
            pltpu.VMEM((n_l // 2, 2 * width, every), bf16),
            pltpu.VMEM((n_l, rows, width), f32),
            dma((n_blocks + len(GROUPS) + 3,)),
            dma((n_l,)),
        ],
    )(
        place, lambdas, squared, level, cross.reshape(2, width, -1), traits,
        *parts,
        *[blocks[b] for b in order],
    )


def solution(mesh):
    split = Mesh(mesh.devices.reshape(8, 8, 4, 2), SAMP + TRAIT)
    return jax.shard_map(
        compute,
        mesh=split,
        in_specs=(P(SAMP, None), P(SAMP, TRAIT), P(None, TRAIT), P(), P()),
        out_specs=P(None, SAMP, TRAIT),
        check_vma=False,
    )
```

```python
import jax
import jax.numpy as jnp
from jax import lax
from jax.experimental import pallas as pl
from jax.experimental.pallas import tpu as pltpu
from jax.sharding import Mesh, PartitionSpec as P


SAMP = ("z", "y")
TRAIT = ("x", "core")
FULL = 67043328
GROUPS = (((0, 0), (0, 1)), ((2, 0), (2, 1)), ((1, 0), (3, 0)))
LAST = ((1, 1), (3, 1))
HBM = pl.BlockSpec(memory_space=pltpu.HBM)
SCALAR = pl.BlockSpec(memory_space=pltpu.SMEM)


def whole(*shape):
    return pl.BlockSpec(shape, lambda *_: (0,) * len(shape))


def call(body, out, in_specs, out_specs, flops, moved, vmem, scratch=(), grid=(1,)):
    return pl.pallas_call(
        body,
        out_shape=out,
        grid=grid,
        in_specs=in_specs,
        out_specs=out_specs,
        scratch_shapes=list(scratch),
        compiler_params=pltpu.CompilerParams(vmem_limit_bytes=vmem),
        cost_estimate=pl.CostEstimate(flops=flops, bytes_accessed=moved, transcendentals=0),
    )


def cross_body(samples, traits, out, samples_v, traits_v, sems):
    n = samples_v.shape[0]
    _, cols = samples_v.shape[1:]
    copies = [pltpu.make_async_copy(traits, traits_v, sems.at[n])]
    for i in range(n):
        copies.append(
            pltpu.make_async_copy(
                samples.at[:, i * cols : (i + 1) * cols], samples_v.at[i], sems.at[i]
            )
        )
    for copy in copies:
        copy.start()
    copies[0].wait()
    flipped = traits_v[...].T
    span = out.shape[2]
    groups = out.shape[0] // 2
    for i in range(n):
        copies[i + 1].wait()
        piece = jnp.dot(flipped, samples_v[i], preferred_element_type=jnp.float32)
        half, at = divmod(i * cols, span)
        out[half * groups : (half + 1) * groups, :, at : at + cols] = piece.astype(
            jnp.bfloat16
        ).reshape(groups, -1, cols)


def sum_body(arrived, out):
    total = arrived[0].astype(jnp.float32)
    for i in range(1, arrived.shape[0]):
        total = total + arrived[i].astype(jnp.float32)
    total = total.astype(jnp.bfloat16)
    for i in range(out.shape[0]):
        out[i] = total


def row_of(place, shift, swap):
    return lax.rem(place[0] + 4 - shift, 4) * 2 + lax.rem(place[1] + swap, 2)


def split(value):
    top = value.astype(jnp.bfloat16)
    return top, value - top.astype(jnp.float32)


def shrink_of(place, squared, lambdas, block, penalties):
    top = squared[pl.ds(row_of(place, *block), 1), :]
    return [top / (top + lambdas[l]) for l in penalties]


def levels(value, place, squared, lambdas, blocks):
    penalties = range(lambdas.shape[0])
    wide = value.astype(jnp.float32)
    high, low = split(wide * wide)
    shrink = jnp.concatenate(
        [
            jnp.concatenate(shrink_of(place, squared, lambdas, block, penalties), axis=0)
            for block in blocks
        ],
        axis=1,
    )
    coarse, fine = split(shrink)
    weight = jnp.concatenate([coarse.astype(jnp.float32), fine], axis=0).astype(jnp.bfloat16)
    return sum(
        lax.dot_general(
            part, weight, (((1,), (1,)), ((), ())), preferred_element_type=jnp.float32
        )
        for part in (high, low.astype(jnp.bfloat16))
    )


def components_body(first, order, *refs):
    n = len(order)
    place, lambdas, squared, samples = refs[:4]
    blocks = refs[4 : 4 + n]
    out, level, samples_v, blocks_v, sems = refs[-5:]
    depth = blocks[0].shape[1]
    n_l = lambdas.shape[0]
    copies = [pltpu.make_async_copy(samples, samples_v, sems.at[n])]
    for i in range(n):
        copies.append(
            pltpu.make_async_copy(
                blocks[i], blocks_v.at[:, i * depth : (i + 1) * depth], sems.at[i]
            )
        )
    for copy in copies:
        copy.start()
    total = jnp.zeros((samples_v.shape[0], 2 * n_l), jnp.float32) if first else refs[4 + n][...]
    copies[0].wait()
    for i in range(0, n, 2):
        copies[i + 1].wait()
        copies[i + 2].wait()
        here = slice(i * depth, (i + 2) * depth)
        value = jnp.dot(
            samples_v[...], blocks_v[:, here], preferred_element_type=jnp.float32
        ).astype(jnp.bfloat16)
        out[:, here] = value
        total = total + levels(value, place, squared, lambdas, order[i : i + 2])
    level[...] = total


def fitted_body(n_groups, order, *refs):
    n = len(order)
    place, lambdas, squared, level, cross, traits, samples = refs[:7]
    parts = refs[7 : 7 + n_groups]
    blocks = refs[7 + n_groups : 7 + n_groups + n]
    out, cross_v, joined, traits_v, samples_v, blocks_v, projected = refs[-11:-4]
    scaled, out_v, sems, out_sems = refs[-4:]
    depth = blocks[0].shape[1]
    width, span = cross.shape[1:]
    pairs = [(cross.at[half], cross_v.at[:, half * span : (half + 1) * span]) for half in range(2)]
    pairs += [(blocks[i], blocks_v.at[:, i * depth : (i + 1) * depth]) for i in range(n)]
    pairs.append((samples, samples_v))
    at = 0
    for part in parts:
        pairs.append((part, joined.at[:, at : at + part.shape[1]]))
        at += part.shape[1]
    pairs.append((traits, traits_v))
    copies = [
        pltpu.make_async_copy(source, target, sems.at[i])
        for i, (source, target) in enumerate(pairs)
    ]
    for copy in copies:
        copy.start()
    copies[0].wait()
    copies[1].wait()
    for i in range(0, n, 2):
        copies[i + 2].wait()
        copies[i + 3].wait()
        here = slice(i * depth, (i + 2) * depth)
        projected[:, here] = jnp.dot(
            cross_v[...], blocks_v[:, here], preferred_element_type=jnp.float32
        ).astype(jnp.bfloat16)
    copies[n + 2].wait()
    here = slice(at, n * depth)
    value = jnp.dot(
        samples_v[...], blocks_v[:, here], preferred_element_type=jnp.float32
    ).astype(jnp.bfloat16)
    joined[:, here] = value
    n_l = lambdas.shape[0]
    total = level[...] + levels(value, place, squared, lambdas, order[at // depth :])
    inverse = 1.0 / jnp.maximum(1.0 - (total[:, :n_l] + total[:, n_l:]), 0.25)
    for copy in copies[n + 3 :]:
        copy.wait()
    results = []
    for pair in range(n_l // 2):
        for i, block in enumerate(order):
            here = slice(i * depth, (i + 1) * depth)
            value = projected[:, here].astype(jnp.float32)
            for j, shrink in enumerate(
                shrink_of(place, squared, lambdas, block, (2 * pair, 2 * pair + 1))
            ):
                scaled[pair, j * width : (j + 1) * width, here] = (value * shrink).astype(
                    jnp.bfloat16
                )
        fitted = lax.dot_general(
            joined[...],
            scaled[pair],
            (((1,), (1,)), ((), ())),
            preferred_element_type=jnp.float32,
        )
        for j in range(2):
            l = 2 * pair + j
            out_v[l] = (
                traits_v[...].astype(jnp.float32) - fitted[:, j * width : (j + 1) * width]
            ) * inverse[:, l : l + 1]
            results.append(pltpu.make_async_copy(out_v.at[l], out.at[l], out_sems.at[l]))
            results[-1].start()
    for copy in results:
        copy.wait()


def compute(samples, traits, whitening, singular, lambdas):
    features, depth = whitening.shape
    rows, width = traits.shape
    n_x, n_core = lax.axis_size("x"), lax.axis_size("core")
    n_samp = lax.axis_size("z") * lax.axis_size("y")
    n_l = lambdas.shape[0]
    every = n_x * n_core * depth
    n_blocks = n_x * n_core
    bf16, f32 = jnp.bfloat16, jnp.float32
    place = jnp.stack([lax.axis_index("x"), lax.axis_index("core")]).astype(jnp.int32)
    squared = (singular * singular).reshape(n_blocks, depth)
    dma = pltpu.SemaphoreType.DMA

    pieces = (n_samp, 2 * width // n_samp, features // 2)
    partial = call(
        cross_body,
        jax.ShapeDtypeStruct(pieces, bf16),
        [HBM, HBM],
        whole(*pieces),
        2 * rows * width * features,
        2 * (rows * width + rows * features + features * width),
        FULL,
        [pltpu.VMEM((8, rows, features // 8), bf16), pltpu.VMEM((rows, width), bf16), dma((9,))],
    )(samples, traits)
    arrived = lax.all_to_all(partial, SAMP, 0, 0)

    shifts = {}
    for shift in (2, 1, 3):
        shifts[shift] = lax.ppermute(whitening, "x", [(i, (i + shift) % n_x) for i in range(n_x)])
    blocks = {(0, 0): whitening}
    for shift in (0, 2, 1, 3):
        if shift:
            blocks[shift, 0] = shifts[shift]
        blocks[shift, 1] = lax.ppermute(blocks[shift, 0], "core", [(0, 1), (1, 0)])

    total = call(
        sum_body,
        jax.ShapeDtypeStruct(pieces, bf16),
        [pl.BlockSpec((*pieces[:2], pieces[2] // 4), lambda i: (0, 0, i))],
        pl.BlockSpec((*pieces[:2], pieces[2] // 4), lambda i: (0, 0, i)),
        features * width,
        4 * features * width,
        FULL,
        grid=(4,),
    )(arrived)
    cross = lax.all_to_all(total, SAMP, 0, 0)

    def components(order, extra):
        n = len(order)
        first = not extra
        columns = 2 * n_l
        return call(
            lambda *refs: components_body(first, order, *refs),
            (
                jax.ShapeDtypeStruct((rows, n * depth), bf16),
                jax.ShapeDtypeStruct((rows, columns), f32),
            ),
            [SCALAR, SCALAR, whole(n_blocks, depth)]
            + [HBM] * (n + 1)
            + [whole(rows, 2 * n_l)] * len(extra),
            (whole(rows, n * depth), whole(rows, columns)),
            2 * rows * features * n * depth,
            2 * (rows * features + features * n * depth + rows * n * depth),
            FULL,
            [
                pltpu.VMEM((rows, features), bf16),
                pltpu.VMEM((features, n * depth), bf16),
                dma((n + 1,)),
            ],
        )(place, lambdas, squared, samples, *[blocks[b] for b in order], *extra)

    parts, state = [], ()
    for group in GROUPS:
        part, level = components(group, state)
        parts.append(part)
        state = (level,)

    order = sum(GROUPS, ()) + LAST
    return call(
        lambda *refs: fitted_body(len(GROUPS), order, *refs),
        jax.ShapeDtypeStruct((n_l, rows, width), f32),
        [SCALAR, SCALAR, whole(n_blocks, depth), whole(rows, 2 * n_l)]
        + [HBM] * (n_blocks + len(GROUPS) + 3),
        HBM,
        2 * n_l * rows * every * width,
        2 * rows * every + 2 * every * width + 4 * n_l * rows * width,
        FULL,
        [
            pltpu.VMEM((width, features), bf16),
            pltpu.VMEM((rows, every), bf16),
            pltpu.VMEM((rows, width), bf16),
            pltpu.VMEM((rows, features), bf16),
            pltpu.VMEM((features, every), bf16),
            pltpu.VMEM((width, every), bf16),
            pltpu.VMEM((n_l // 2, 2 * width, every), bf16),
            pltpu.VMEM((n_l, rows, width), f32),
            dma((n_blocks + len(GROUPS) + 4,)),
            dma((n_l,)),
        ],
    )(
        place, lambdas, squared, level, cross.reshape(2, width, -1), traits, samples,
        *parts,
        *[blocks[b] for b in order],
    )


def solution(mesh):
    split = Mesh(mesh.devices.reshape(8, 8, 4, 2), SAMP + TRAIT)
    return jax.shard_map(
        compute,
        mesh=split,
        in_specs=(P(SAMP, None), P(SAMP, TRAIT), P(None, TRAIT), P(), P()),
        out_specs=P(None, SAMP, TRAIT),
        check_vma=False,
    )
```

```python
import jax
import jax.numpy as jnp
from jax import lax
from jax.experimental import pallas as pl
from jax.experimental.pallas import tpu as pltpu
from jax.sharding import Mesh, PartitionSpec as P


SAMP = ("z", "y")
TRAIT = ("x", "core")
FULL = 67043328
GROUPS = (((0, 0), (0, 1)), ((2, 0), (2, 1)), ((1, 0), (3, 0)))
LAST = ((1, 1), (3, 1))
HBM = pl.BlockSpec(memory_space=pltpu.HBM)
SCALAR = pl.BlockSpec(memory_space=pltpu.SMEM)


def whole(*shape):
    return pl.BlockSpec(shape, lambda *_: (0,) * len(shape))


def call(body, out, in_specs, out_specs, flops, moved, vmem, scratch=(), grid=(1,)):
    return pl.pallas_call(
        body,
        out_shape=out,
        grid=grid,
        in_specs=in_specs,
        out_specs=out_specs,
        scratch_shapes=list(scratch),
        compiler_params=pltpu.CompilerParams(vmem_limit_bytes=vmem),
        cost_estimate=pl.CostEstimate(flops=flops, bytes_accessed=moved, transcendentals=0),
    )


def cross_body(samples, traits, out, samples_v, traits_v, out_v, sems, out_sems):
    n = samples_v.shape[0]
    _, cols = samples_v.shape[1:]
    copies = [pltpu.make_async_copy(traits, traits_v, sems.at[n])]
    for i in range(n):
        copies.append(
            pltpu.make_async_copy(
                samples.at[:, i * cols : (i + 1) * cols], samples_v.at[i], sems.at[i]
            )
        )
    for copy in copies:
        copy.start()
    copies[0].wait()
    flipped = traits_v[...].T
    span = out.shape[2]
    groups = out.shape[0] // 2
    results = []
    for i in range(n):
        copies[i + 1].wait()
        piece = jnp.dot(flipped, samples_v[i], preferred_element_type=jnp.float32)
        out_v[i] = piece.astype(jnp.bfloat16).reshape(groups, -1, cols)
        half, at = divmod(i * cols, span)
        results.append(
            pltpu.make_async_copy(
                out_v.at[i],
                out.at[half * groups : (half + 1) * groups, :, at : at + cols],
                out_sems.at[i],
            )
        )
        results[-1].start()
    for copy in results:
        copy.wait()


def sum_body(arrived, out, arrived_v, out_v, sems, out_sems):
    n = sems.shape[0]
    part = arrived.shape[0] // n
    copies = [
        pltpu.make_async_copy(
            arrived.at[i * part : (i + 1) * part],
            arrived_v.at[i * part : (i + 1) * part],
            sems.at[i],
        )
        for i in range(n)
    ]
    for copy in copies:
        copy.start()
    total = 0.0
    for i in range(n):
        copies[i].wait()
        for j in range(i * part, (i + 1) * part):
            total = total + arrived_v[j].astype(jnp.float32)
    total = total.astype(jnp.bfloat16)
    for i in range(part):
        out_v[i] = total
    results = [
        pltpu.make_async_copy(out_v, out.at[i * part : (i + 1) * part], out_sems.at[i])
        for i in range(n)
    ]
    for copy in results:
        copy.start()
    for copy in results:
        copy.wait()


def row_of(place, shift, swap):
    return lax.rem(place[0] + 4 - shift, 4) * 2 + lax.rem(place[1] + swap, 2)


def split(value):
    top = value.astype(jnp.bfloat16)
    return top, value - top.astype(jnp.float32)


def shrink_of(place, squared, lambdas, block, penalties):
    top = squared[pl.ds(row_of(place, *block), 1), :]
    return [top / (top + lambdas[l]) for l in penalties]


def levels(value, place, squared, lambdas, blocks):
    penalties = range(lambdas.shape[0])
    wide = value.astype(jnp.float32)
    high, low = split(wide * wide)
    shrink = jnp.concatenate(
        [
            jnp.concatenate(shrink_of(place, squared, lambdas, block, penalties), axis=0)
            for block in blocks
        ],
        axis=1,
    )
    coarse, fine = split(shrink)
    weight = jnp.concatenate([coarse.astype(jnp.float32), fine], axis=0).astype(jnp.bfloat16)
    return sum(
        lax.dot_general(
            part, weight, (((1,), (1,)), ((), ())), preferred_element_type=jnp.float32
        )
        for part in (high, low.astype(jnp.bfloat16))
    )


def components_body(first, order, *refs):
    n = len(order)
    place, lambdas, squared, samples = refs[:4]
    blocks = refs[4 : 4 + n]
    out, level, samples_v, blocks_v, sems = refs[-5:]
    depth = blocks[0].shape[1]
    n_l = lambdas.shape[0]
    copies = [pltpu.make_async_copy(samples, samples_v, sems.at[n])]
    for i in range(n):
        copies.append(
            pltpu.make_async_copy(
                blocks[i], blocks_v.at[:, i * depth : (i + 1) * depth], sems.at[i]
            )
        )
    for copy in copies:
        copy.start()
    total = jnp.zeros((samples_v.shape[0], 2 * n_l), jnp.float32) if first else refs[4 + n][...]
    copies[0].wait()
    for i in range(0, n, 2):
        copies[i + 1].wait()
        copies[i + 2].wait()
        here = slice(i * depth, (i + 2) * depth)
        value = jnp.dot(
            samples_v[...], blocks_v[:, here], preferred_element_type=jnp.float32
        ).astype(jnp.bfloat16)
        out[:, here] = value
        total = total + levels(value, place, squared, lambdas, order[i : i + 2])
    level[...] = total


def fitted_body(n_groups, order, *refs):
    n = len(order)
    place, lambdas, squared, level, cross, traits, samples = refs[:7]
    parts = refs[7 : 7 + n_groups]
    blocks = refs[7 + n_groups : 7 + n_groups + n]
    out, cross_v, joined, traits_v, samples_v, blocks_v = refs[-10:-4]
    scaled, out_v, sems, out_sems = refs[-4:]
    depth = blocks[0].shape[1]
    width, span = cross.shape[1:]
    n_l = lambdas.shape[0]
    pairs = [(cross.at[half], cross_v.at[:, half * span : (half + 1) * span]) for half in range(2)]
    pairs += [(blocks[i], blocks_v.at[:, i * depth : (i + 1) * depth]) for i in range(n)]
    pairs.append((samples, samples_v))
    at = 0
    for part in parts:
        pairs.append((part, joined.at[:, at : at + part.shape[1]]))
        at += part.shape[1]
    pairs.append((traits, traits_v))
    copies = [
        pltpu.make_async_copy(source, target, sems.at[i])
        for i, (source, target) in enumerate(pairs)
    ]
    for copy in copies:
        copy.start()
    copies[0].wait()
    copies[1].wait()
    for i in range(0, n, 2):
        copies[i + 2].wait()
        copies[i + 3].wait()
        here = slice(i * depth, (i + 2) * depth)
        value = jnp.dot(cross_v[...], blocks_v[:, here], preferred_element_type=jnp.float32)
        value = value.astype(jnp.bfloat16).astype(jnp.float32)
        for j, block in enumerate(order[i : i + 2]):
            columns = slice((i + j) * depth, (i + j + 1) * depth)
            for l, shrink in enumerate(shrink_of(place, squared, lambdas, block, range(n_l))):
                scaled[l * width : (l + 1) * width, columns] = (
                    value[:, j * depth : (j + 1) * depth] * shrink
                ).astype(jnp.bfloat16)
    copies[n + 2].wait()
    here = slice(at, n * depth)
    value = jnp.dot(
        samples_v[...], blocks_v[:, here], preferred_element_type=jnp.float32
    ).astype(jnp.bfloat16)
    joined[:, here] = value
    total = level[...] + levels(value, place, squared, lambdas, order[at // depth :])
    inverse = 1.0 / jnp.maximum(1.0 - (total[:, :n_l] + total[:, n_l:]), 0.25)
    for copy in copies[n + 3 :]:
        copy.wait()
    results = []
    for pair in range(n_l // 2):
        fitted = lax.dot_general(
            joined[...],
            scaled[2 * pair * width : 2 * (pair + 1) * width],
            (((1,), (1,)), ((), ())),
            preferred_element_type=jnp.float32,
        )
        for j in range(2):
            l = 2 * pair + j
            out_v[l] = (
                traits_v[...].astype(jnp.float32) - fitted[:, j * width : (j + 1) * width]
            ) * inverse[:, l : l + 1]
            results.append(pltpu.make_async_copy(out_v.at[l], out.at[l], out_sems.at[l]))
            results[-1].start()
    for copy in results:
        copy.wait()


def compute(samples, traits, whitening, singular, lambdas):
    features, depth = whitening.shape
    rows, width = traits.shape
    n_x, n_core = lax.axis_size("x"), lax.axis_size("core")
    n_samp = lax.axis_size("z") * lax.axis_size("y")
    n_l = lambdas.shape[0]
    every = n_x * n_core * depth
    n_blocks = n_x * n_core
    bf16, f32 = jnp.bfloat16, jnp.float32
    place = jnp.stack([lax.axis_index("x"), lax.axis_index("core")]).astype(jnp.int32)
    squared = (singular * singular).reshape(n_blocks, depth)
    dma = pltpu.SemaphoreType.DMA

    pieces = (n_samp, 2 * width // n_samp, features // 2)
    partial = call(
        cross_body,
        jax.ShapeDtypeStruct(pieces, bf16),
        [HBM, HBM],
        HBM,
        2 * rows * width * features,
        2 * (rows * width + rows * features + features * width),
        FULL,
        [
            pltpu.VMEM((4, rows, features // 4), bf16),
            pltpu.VMEM((rows, width), bf16),
            pltpu.VMEM((4, pieces[0] // 2, pieces[1], features // 4), bf16),
            dma((5,)),
            dma((4,)),
        ],
    )(samples, traits)
    arrived = lax.all_to_all(partial, SAMP, 0, 0)

    shifts = {}
    for shift in (2, 1, 3):
        shifts[shift] = lax.ppermute(whitening, "x", [(i, (i + shift) % n_x) for i in range(n_x)])
    blocks = {(0, 0): whitening}
    for shift in (0, 2, 1, 3):
        if shift:
            blocks[shift, 0] = shifts[shift]
        blocks[shift, 1] = lax.ppermute(blocks[shift, 0], "core", [(0, 1), (1, 0)])

    total = call(
        sum_body,
        jax.ShapeDtypeStruct(pieces, bf16),
        [HBM],
        HBM,
        features * width,
        4 * features * width,
        FULL,
        [
            pltpu.VMEM(pieces, bf16),
            pltpu.VMEM((pieces[0] // 4, *pieces[1:]), bf16),
            dma((4,)),
            dma((4,)),
        ],
    )(arrived)
    cross = lax.all_to_all(total, SAMP, 0, 0)

    def components(order, extra):
        n = len(order)
        first = not extra
        columns = 2 * n_l
        return call(
            lambda *refs: components_body(first, order, *refs),
            (
                jax.ShapeDtypeStruct((rows, n * depth), bf16),
                jax.ShapeDtypeStruct((rows, columns), f32),
            ),
            [SCALAR, SCALAR, whole(n_blocks, depth)]
            + [HBM] * (n + 1)
            + [whole(rows, 2 * n_l)] * len(extra),
            (whole(rows, n * depth), whole(rows, columns)),
            2 * rows * features * n * depth,
            2 * (rows * features + features * n * depth + rows * n * depth),
            FULL,
            [
                pltpu.VMEM((rows, features), bf16),
                pltpu.VMEM((features, n * depth), bf16),
                dma((n + 1,)),
            ],
        )(place, lambdas, squared, samples, *[blocks[b] for b in order], *extra)

    parts, state = [], ()
    for group in GROUPS:
        part, level = components(group, state)
        parts.append(part)
        state = (level,)

    order = sum(GROUPS, ()) + LAST
    return call(
        lambda *refs: fitted_body(len(GROUPS), order, *refs),
        jax.ShapeDtypeStruct((n_l, rows, width), f32),
        [SCALAR, SCALAR, whole(n_blocks, depth), whole(rows, 2 * n_l)]
        + [HBM] * (n_blocks + len(GROUPS) + 3),
        HBM,
        2 * n_l * rows * every * width,
        2 * rows * every + 2 * every * width + 4 * n_l * rows * width,
        FULL,
        [
            pltpu.VMEM((width, features), bf16),
            pltpu.VMEM((rows, every), bf16),
            pltpu.VMEM((rows, width), bf16),
            pltpu.VMEM((rows, features), bf16),
            pltpu.VMEM((features, every), bf16),
            pltpu.VMEM((n_l * width, every), bf16),
            pltpu.VMEM((n_l, rows, width), f32),
            dma((n_blocks + len(GROUPS) + 4,)),
            dma((n_l,)),
        ],
    )(
        place, lambdas, squared, level, cross.reshape(2, width, -1), traits, samples,
        *parts,
        *[blocks[b] for b in order],
    )


def solution(mesh):
    split = Mesh(mesh.devices.reshape(8, 8, 4, 2), SAMP + TRAIT)
    return jax.shard_map(
        compute,
        mesh=split,
        in_specs=(P(SAMP, None), P(SAMP, TRAIT), P(None, TRAIT), P(), P()),
        out_specs=P(None, SAMP, TRAIT),
        check_vma=False,
    )
```

```python
import jax
import jax.numpy as jnp
from jax import lax
from jax.experimental import pallas as pl
from jax.experimental.pallas import tpu as pltpu
from jax.sharding import Mesh, PartitionSpec as P


SAMP = ("z", "y")
TRAIT = ("x", "core")
FULL = 67043328
GROUPS = (((0, 0), (0, 1)), ((2, 0), (2, 1)), ((1, 0), (3, 0)))
LAST = ((1, 1), (3, 1))
HBM = pl.BlockSpec(memory_space=pltpu.HBM)
SCALAR = pl.BlockSpec(memory_space=pltpu.SMEM)


def whole(*shape):
    return pl.BlockSpec(shape, lambda *_: (0,) * len(shape))


def call(body, out, in_specs, out_specs, flops, moved, vmem, scratch=(), grid=(1,)):
    return pl.pallas_call(
        body,
        out_shape=out,
        grid=grid,
        in_specs=in_specs,
        out_specs=out_specs,
        scratch_shapes=list(scratch),
        compiler_params=pltpu.CompilerParams(vmem_limit_bytes=vmem),
        cost_estimate=pl.CostEstimate(flops=flops, bytes_accessed=moved, transcendentals=0),
    )


def cross_body(samples, traits, out, samples_v, traits_v, out_v, sems, out_sems):
    n = samples_v.shape[0]
    _, cols = samples_v.shape[1:]
    copies = [pltpu.make_async_copy(traits, traits_v, sems.at[n])]
    for i in range(n):
        copies.append(
            pltpu.make_async_copy(
                samples.at[:, i * cols : (i + 1) * cols], samples_v.at[i], sems.at[i]
            )
        )
    for copy in copies:
        copy.start()
    copies[0].wait()
    flipped = traits_v[...].T
    span = out.shape[2]
    groups = out.shape[0] // 2
    results = []
    for i in range(n):
        copies[i + 1].wait()
        piece = jnp.dot(flipped, samples_v[i], preferred_element_type=jnp.float32)
        out_v[i] = piece.astype(jnp.bfloat16).reshape(groups, -1, cols)
        half, at = divmod(i * cols, span)
        results.append(
            pltpu.make_async_copy(
                out_v.at[i],
                out.at[half * groups : (half + 1) * groups, :, at : at + cols],
                out_sems.at[i],
            )
        )
        results[-1].start()
    for copy in results:
        copy.wait()


def sum_body(arrived, out, arrived_v, out_v, sems, out_sems):
    n = sems.shape[0]
    part = arrived.shape[0] // n
    copies = [
        pltpu.make_async_copy(
            arrived.at[i * part : (i + 1) * part],
            arrived_v.at[i * part : (i + 1) * part],
            sems.at[i],
        )
        for i in range(n)
    ]
    for copy in copies:
        copy.start()
    total = 0.0
    for i in range(n):
        copies[i].wait()
        for j in range(i * part, (i + 1) * part):
            total = total + arrived_v[j].astype(jnp.float32)
    total = total.astype(jnp.bfloat16)
    for i in range(part):
        out_v[i] = total
    results = [
        pltpu.make_async_copy(out_v, out.at[i * part : (i + 1) * part], out_sems.at[i])
        for i in range(n)
    ]
    for copy in results:
        copy.start()
    for copy in results:
        copy.wait()


def row_of(place, shift, swap):
    return lax.rem(place[0] + 4 - shift, 4) * 2 + lax.rem(place[1] + swap, 2)


def split(value):
    top = value.astype(jnp.bfloat16)
    return top, value - top.astype(jnp.float32)


def shrink_of(place, squared, lambdas, block, penalties):
    top = squared[pl.ds(row_of(place, *block), 1), :]
    return [top / (top + lambdas[l]) for l in penalties]


def levels(value, place, squared, lambdas, blocks):
    penalties = range(lambdas.shape[0])
    wide = value.astype(jnp.float32)
    high, low = split(wide * wide)
    shrink = jnp.concatenate(
        [
            jnp.concatenate(shrink_of(place, squared, lambdas, block, penalties), axis=0)
            for block in blocks
        ],
        axis=1,
    )
    coarse, fine = split(shrink)
    weight = jnp.concatenate([coarse.astype(jnp.float32), fine], axis=0).astype(jnp.bfloat16)
    return sum(
        lax.dot_general(
            part, weight, (((1,), (1,)), ((), ())), preferred_element_type=jnp.float32
        )
        for part in (high, low.astype(jnp.bfloat16))
    )


def components_body(first, order, *refs):
    n = len(order)
    place, lambdas, squared, samples = refs[:4]
    blocks = refs[4 : 4 + n]
    out, level, samples_v, blocks_v, sems = refs[-5:]
    depth = blocks[0].shape[1]
    n_l = lambdas.shape[0]
    copies = [pltpu.make_async_copy(samples, samples_v, sems.at[n])]
    for i in range(n):
        copies.append(
            pltpu.make_async_copy(
                blocks[i], blocks_v.at[:, i * depth : (i + 1) * depth], sems.at[i]
            )
        )
    for copy in copies:
        copy.start()
    total = jnp.zeros((samples_v.shape[0], 2 * n_l), jnp.float32) if first else refs[4 + n][...]
    copies[0].wait()
    for i in range(0, n, 2):
        copies[i + 1].wait()
        copies[i + 2].wait()
        here = slice(i * depth, (i + 2) * depth)
        value = jnp.dot(
            samples_v[...], blocks_v[:, here], preferred_element_type=jnp.float32
        ).astype(jnp.bfloat16)
        out[:, here] = value
        total = total + levels(value, place, squared, lambdas, order[i : i + 2])
    level[...] = total


def fitted_body(n_groups, order, *refs):
    n = len(order)
    place, lambdas, squared, level, cross, traits, samples = refs[:7]
    parts = refs[7 : 7 + n_groups]
    blocks = refs[7 + n_groups : 7 + n_groups + n]
    out, cross_v, joined, traits_v, samples_v, blocks_v = refs[-10:-4]
    scaled, out_v, sems, out_sems = refs[-4:]
    depth = blocks[0].shape[1]
    width, span = cross.shape[1:]
    n_l = lambdas.shape[0]
    pairs = [(cross.at[half], cross_v.at[:, half * span : (half + 1) * span]) for half in range(2)]
    pairs += [(blocks[i], blocks_v.at[:, i * depth : (i + 1) * depth]) for i in range(n)]
    pairs.append((samples, samples_v))
    at = 0
    for part in parts:
        pairs.append((part, joined.at[:, at : at + part.shape[1]]))
        at += part.shape[1]
    pairs.append((traits, traits_v))
    copies = [
        pltpu.make_async_copy(source, target, sems.at[i])
        for i, (source, target) in enumerate(pairs)
    ]
    stages = (copies[6:8], copies[8 : n + 3], copies[n + 3 :])
    for copy in copies[:6]:
        copy.start()
    copies[0].wait()
    copies[1].wait()
    for i in range(0, n, 2):
        copies[i + 2].wait()
        copies[i + 3].wait()
        if i // 2 < len(stages):
            for copy in stages[i // 2]:
                copy.start()
        here = slice(i * depth, (i + 2) * depth)
        value = jnp.dot(cross_v[...], blocks_v[:, here], preferred_element_type=jnp.float32)
        value = value.astype(jnp.bfloat16).astype(jnp.float32)
        for j, block in enumerate(order[i : i + 2]):
            columns = slice((i + j) * depth, (i + j + 1) * depth)
            for l, shrink in enumerate(shrink_of(place, squared, lambdas, block, range(n_l))):
                scaled[l * width : (l + 1) * width, columns] = (
                    value[:, j * depth : (j + 1) * depth] * shrink
                ).astype(jnp.bfloat16)
    copies[n + 2].wait()
    here = slice(at, n * depth)
    value = jnp.dot(
        samples_v[...], blocks_v[:, here], preferred_element_type=jnp.float32
    ).astype(jnp.bfloat16)
    joined[:, here] = value
    total = level[...] + levels(value, place, squared, lambdas, order[at // depth :])
    inverse = 1.0 / jnp.maximum(1.0 - (total[:, :n_l] + total[:, n_l:]), 0.25)
    for copy in copies[n + 3 :]:
        copy.wait()
    results = []
    for pair in range(n_l // 2):
        fitted = lax.dot_general(
            joined[...],
            scaled[2 * pair * width : 2 * (pair + 1) * width],
            (((1,), (1,)), ((), ())),
            preferred_element_type=jnp.float32,
        )
        for j in range(2):
            l = 2 * pair + j
            out_v[l] = (
                traits_v[...].astype(jnp.float32) - fitted[:, j * width : (j + 1) * width]
            ) * inverse[:, l : l + 1]
            results.append(pltpu.make_async_copy(out_v.at[l], out.at[l], out_sems.at[l]))
            results[-1].start()
    for copy in results:
        copy.wait()


def compute(samples, traits, whitening, singular, lambdas):
    features, depth = whitening.shape
    rows, width = traits.shape
    n_x, n_core = lax.axis_size("x"), lax.axis_size("core")
    n_samp = lax.axis_size("z") * lax.axis_size("y")
    n_l = lambdas.shape[0]
    every = n_x * n_core * depth
    n_blocks = n_x * n_core
    bf16, f32 = jnp.bfloat16, jnp.float32
    place = jnp.stack([lax.axis_index("x"), lax.axis_index("core")]).astype(jnp.int32)
    squared = (singular * singular).reshape(n_blocks, depth)
    dma = pltpu.SemaphoreType.DMA

    pieces = (n_samp, 2 * width // n_samp, features // 2)
    partial = call(
        cross_body,
        jax.ShapeDtypeStruct(pieces, bf16),
        [HBM, HBM],
        HBM,
        2 * rows * width * features,
        2 * (rows * width + rows * features + features * width),
        FULL,
        [
            pltpu.VMEM((4, rows, features // 4), bf16),
            pltpu.VMEM((rows, width), bf16),
            pltpu.VMEM((4, pieces[0] // 2, pieces[1], features // 4), bf16),
            dma((5,)),
            dma((4,)),
        ],
    )(samples, traits)
    arrived = lax.all_to_all(partial, SAMP, 0, 0)

    shifts = {}
    for shift in (2, 1, 3):
        shifts[shift] = lax.ppermute(whitening, "x", [(i, (i + shift) % n_x) for i in range(n_x)])
    blocks = {(0, 0): whitening}
    for shift in (0, 2, 1, 3):
        if shift:
            blocks[shift, 0] = shifts[shift]
        blocks[shift, 1] = lax.ppermute(blocks[shift, 0], "core", [(0, 1), (1, 0)])

    total = call(
        sum_body,
        jax.ShapeDtypeStruct(pieces, bf16),
        [HBM],
        HBM,
        features * width,
        4 * features * width,
        FULL,
        [
            pltpu.VMEM(pieces, bf16),
            pltpu.VMEM((pieces[0] // 4, *pieces[1:]), bf16),
            dma((4,)),
            dma((4,)),
        ],
    )(arrived)
    cross = lax.all_to_all(total, SAMP, 0, 0)

    def components(order, extra):
        n = len(order)
        first = not extra
        columns = 2 * n_l
        return call(
            lambda *refs: components_body(first, order, *refs),
            (
                jax.ShapeDtypeStruct((rows, n * depth), bf16),
                jax.ShapeDtypeStruct((rows, columns), f32),
            ),
            [SCALAR, SCALAR, whole(n_blocks, depth)]
            + [HBM] * (n + 1)
            + [whole(rows, 2 * n_l)] * len(extra),
            (whole(rows, n * depth), whole(rows, columns)),
            2 * rows * features * n * depth,
            2 * (rows * features + features * n * depth + rows * n * depth),
            FULL,
            [
                pltpu.VMEM((rows, features), bf16),
                pltpu.VMEM((features, n * depth), bf16),
                dma((n + 1,)),
            ],
        )(place, lambdas, squared, samples, *[blocks[b] for b in order], *extra)

    parts, state = [], ()
    for group in GROUPS:
        part, level = components(group, state)
        parts.append(part)
        state = (level,)

    order = sum(GROUPS, ()) + LAST
    return call(
        lambda *refs: fitted_body(len(GROUPS), order, *refs),
        jax.ShapeDtypeStruct((n_l, rows, width), f32),
        [SCALAR, SCALAR, whole(n_blocks, depth), whole(rows, 2 * n_l)]
        + [HBM] * (n_blocks + len(GROUPS) + 3),
        HBM,
        2 * n_l * rows * every * width,
        2 * rows * every + 2 * every * width + 4 * n_l * rows * width,
        FULL,
        [
            pltpu.VMEM((width, features), bf16),
            pltpu.VMEM((rows, every), bf16),
            pltpu.VMEM((rows, width), bf16),
            pltpu.VMEM((rows, features), bf16),
            pltpu.VMEM((features, every), bf16),
            pltpu.VMEM((n_l * width, every), bf16),
            pltpu.VMEM((n_l, rows, width), f32),
            dma((n_blocks + len(GROUPS) + 4,)),
            dma((n_l,)),
        ],
    )(
        place, lambdas, squared, level, cross.reshape(2, width, -1), traits, samples,
        *parts,
        *[blocks[b] for b in order],
    )


def solution(mesh):
    split = Mesh(mesh.devices.reshape(8, 8, 4, 2), SAMP + TRAIT)
    return jax.shard_map(
        compute,
        mesh=split,
        in_specs=(P(SAMP, None), P(SAMP, TRAIT), P(None, TRAIT), P(), P()),
        out_specs=P(None, SAMP, TRAIT),
        check_vma=False,
    )
```

```python
import jax
import jax.numpy as jnp
from jax import lax
from jax.experimental import pallas as pl
from jax.experimental.pallas import tpu as pltpu
from jax.sharding import Mesh, PartitionSpec as P


SAMP = ("z", "y")
TRAIT = ("x", "core")
FULL = 67043328
GROUPS = (((0, 0), (0, 1)), ((2, 0), (2, 1)), ((1, 0), (3, 0)))
LAST = ((1, 1), (3, 1))
HBM = pl.BlockSpec(memory_space=pltpu.HBM)
SCALAR = pl.BlockSpec(memory_space=pltpu.SMEM)


def whole(*shape):
    return pl.BlockSpec(shape, lambda *_: (0,) * len(shape))


def call(body, out, in_specs, out_specs, flops, moved, vmem, scratch=(), grid=(1,)):
    return pl.pallas_call(
        body,
        out_shape=out,
        grid=grid,
        in_specs=in_specs,
        out_specs=out_specs,
        scratch_shapes=list(scratch),
        compiler_params=pltpu.CompilerParams(vmem_limit_bytes=vmem),
        cost_estimate=pl.CostEstimate(flops=flops, bytes_accessed=moved, transcendentals=0),
    )


def cross_body(samples, traits, out, samples_v, traits_v, out_v, sems, out_sems):
    n = samples_v.shape[0]
    _, cols = samples_v.shape[1:]
    copies = [pltpu.make_async_copy(traits, traits_v, sems.at[n])]
    for i in range(n):
        copies.append(
            pltpu.make_async_copy(
                samples.at[:, i * cols : (i + 1) * cols], samples_v.at[i], sems.at[i]
            )
        )
    for copy in copies:
        copy.start()
    copies[0].wait()
    flipped = traits_v[...].T
    span = out.shape[2]
    groups = out.shape[0] // 2
    results = []
    for i in range(n):
        copies[i + 1].wait()
        piece = jnp.dot(flipped, samples_v[i], preferred_element_type=jnp.float32)
        out_v[i] = piece.astype(jnp.bfloat16).reshape(groups, -1, cols)
        half, at = divmod(i * cols, span)
        results.append(
            pltpu.make_async_copy(
                out_v.at[i],
                out.at[half * groups : (half + 1) * groups, :, at : at + cols],
                out_sems.at[i],
            )
        )
        results[-1].start()
    for copy in results:
        copy.wait()


def sum_body(arrived, out, arrived_v, out_v, sems, out_sems):
    n = sems.shape[0]
    part = arrived.shape[0] // n
    copies = [
        pltpu.make_async_copy(
            arrived.at[i * part : (i + 1) * part],
            arrived_v.at[i * part : (i + 1) * part],
            sems.at[i],
        )
        for i in range(n)
    ]
    for copy in copies:
        copy.start()
    total = 0.0
    for i in range(n):
        copies[i].wait()
        for j in range(i * part, (i + 1) * part):
            total = total + arrived_v[j].astype(jnp.float32)
    total = total.astype(jnp.bfloat16)
    for i in range(part):
        out_v[i] = total
    results = [
        pltpu.make_async_copy(out_v, out.at[i * part : (i + 1) * part], out_sems.at[i])
        for i in range(n)
    ]
    for copy in results:
        copy.start()
    for copy in results:
        copy.wait()


def row_of(place, shift, swap):
    return lax.rem(place[0] + 4 - shift, 4) * 2 + lax.rem(place[1] + swap, 2)


def split(value):
    top = value.astype(jnp.bfloat16)
    return top, value - top.astype(jnp.float32)


def shrink_of(place, squared, lambdas, block, penalties):
    top = squared[pl.ds(row_of(place, *block), 1), :]
    return [top / (top + lambdas[l]) for l in penalties]


def levels(value, place, squared, lambdas, blocks):
    penalties = range(lambdas.shape[0])
    wide = value.astype(jnp.float32)
    high, low = split(wide * wide)
    shrink = jnp.concatenate(
        [
            jnp.concatenate(shrink_of(place, squared, lambdas, block, penalties), axis=0)
            for block in blocks
        ],
        axis=1,
    )
    coarse, fine = split(shrink)
    weight = jnp.concatenate([coarse.astype(jnp.float32), fine], axis=0).astype(jnp.bfloat16)
    return sum(
        lax.dot_general(
            part, weight, (((1,), (1,)), ((), ())), preferred_element_type=jnp.float32
        )
        for part in (high, low.astype(jnp.bfloat16))
    )


def components_body(first, order, *refs):
    n = len(order)
    place, lambdas, squared, samples = refs[:4]
    blocks = refs[4 : 4 + n]
    out, level, samples_v, blocks_v, sems = refs[-5:]
    depth = blocks[0].shape[1]
    n_l = lambdas.shape[0]
    copies = [pltpu.make_async_copy(samples, samples_v, sems.at[n])]
    for i in range(n):
        copies.append(
            pltpu.make_async_copy(
                blocks[i], blocks_v.at[:, i * depth : (i + 1) * depth], sems.at[i]
            )
        )
    for copy in copies:
        copy.start()
    total = jnp.zeros((samples_v.shape[0], 2 * n_l), jnp.float32) if first else refs[4 + n][...]
    copies[0].wait()
    for i in range(0, n, 2):
        copies[i + 1].wait()
        copies[i + 2].wait()
        here = slice(i * depth, (i + 2) * depth)
        value = jnp.dot(
            samples_v[...], blocks_v[:, here], preferred_element_type=jnp.float32
        ).astype(jnp.bfloat16)
        out[:, here] = value
        total = total + levels(value, place, squared, lambdas, order[i : i + 2])
    level[...] = total


def fitted_body(n_groups, order, *refs):
    n = len(order)
    place, lambdas, squared, level, cross, traits, samples = refs[:7]
    parts = refs[7 : 7 + n_groups]
    blocks = refs[7 + n_groups : 7 + n_groups + n]
    out, stacked, joined, traits_v, blocks_v, projected = refs[-10:-4]
    scaled, out_v, sems, out_sems = refs[-4:]
    depth = blocks[0].shape[1]
    width, span = cross.shape[1:]
    pairs = [
        (cross.at[half], stacked.at[:width, half * span : (half + 1) * span]) for half in range(2)
    ]
    pairs += [(blocks[i], blocks_v.at[:, i * depth : (i + 1) * depth]) for i in range(n)]
    pairs.append((samples, stacked.at[width:, :]))
    at = 0
    for part in parts:
        pairs.append((part, joined.at[:, at : at + part.shape[1]]))
        at += part.shape[1]
    pairs.append((traits, traits_v))
    copies = [
        pltpu.make_async_copy(source, target, sems.at[i])
        for i, (source, target) in enumerate(pairs)
    ]
    for copy in copies:
        copy.start()
    copies[0].wait()
    copies[1].wait()
    for i in range(0, n, 2):
        copies[i + 2].wait()
        copies[i + 3].wait()
        here = slice(i * depth, (i + 2) * depth)
        last = i == n - 2
        if last:
            for copy in copies[n + 2 :]:
                copy.wait()
        value = jnp.dot(
            stacked[...] if last else stacked[:width, :],
            blocks_v[:, here],
            preferred_element_type=jnp.float32,
        ).astype(jnp.bfloat16)
        projected[:, here] = value[:width]
        if last:
            value = value[width:]
            joined[:, here] = value
    n_l = lambdas.shape[0]
    total = level[...] + levels(value, place, squared, lambdas, order[at // depth :])
    inverse = 1.0 / jnp.maximum(1.0 - (total[:, :n_l] + total[:, n_l:]), 0.25)
    results = []
    for pair in range(n_l // 2):
        for i, block in enumerate(order):
            here = slice(i * depth, (i + 1) * depth)
            value = projected[:, here].astype(jnp.float32)
            for j, shrink in enumerate(
                shrink_of(place, squared, lambdas, block, (2 * pair, 2 * pair + 1))
            ):
                scaled[pair, j * width : (j + 1) * width, here] = (value * shrink).astype(
                    jnp.bfloat16
                )
        fitted = lax.dot_general(
            joined[...],
            scaled[pair],
            (((1,), (1,)), ((), ())),
            preferred_element_type=jnp.float32,
        )
        for j in range(2):
            l = 2 * pair + j
            out_v[l] = (
                traits_v[...].astype(jnp.float32) - fitted[:, j * width : (j + 1) * width]
            ) * inverse[:, l : l + 1]
            results.append(pltpu.make_async_copy(out_v.at[l], out.at[l], out_sems.at[l]))
            results[-1].start()
    for copy in results:
        copy.wait()


def compute(samples, traits, whitening, singular, lambdas):
    features, depth = whitening.shape
    rows, width = traits.shape
    n_x, n_core = lax.axis_size("x"), lax.axis_size("core")
    n_samp = lax.axis_size("z") * lax.axis_size("y")
    n_l = lambdas.shape[0]
    every = n_x * n_core * depth
    n_blocks = n_x * n_core
    bf16, f32 = jnp.bfloat16, jnp.float32
    place = jnp.stack([lax.axis_index("x"), lax.axis_index("core")]).astype(jnp.int32)
    squared = (singular * singular).reshape(n_blocks, depth)
    dma = pltpu.SemaphoreType.DMA

    pieces = (n_samp, 2 * width // n_samp, features // 2)
    partial = call(
        cross_body,
        jax.ShapeDtypeStruct(pieces, bf16),
        [HBM, HBM],
        HBM,
        2 * rows * width * features,
        2 * (rows * width + rows * features + features * width),
        FULL,
        [
            pltpu.VMEM((4, rows, features // 4), bf16),
            pltpu.VMEM((rows, width), bf16),
            pltpu.VMEM((4, pieces[0] // 2, pieces[1], features // 4), bf16),
            dma((5,)),
            dma((4,)),
        ],
    )(samples, traits)
    arrived = lax.all_to_all(partial, SAMP, 0, 0)

    shifts = {}
    for shift in (2, 1, 3):
        shifts[shift] = lax.ppermute(whitening, "x", [(i, (i + shift) % n_x) for i in range(n_x)])
    blocks = {(0, 0): whitening}
    for shift in (0, 2, 1, 3):
        if shift:
            blocks[shift, 0] = shifts[shift]
        blocks[shift, 1] = lax.ppermute(blocks[shift, 0], "core", [(0, 1), (1, 0)])

    total = call(
        sum_body,
        jax.ShapeDtypeStruct(pieces, bf16),
        [HBM],
        HBM,
        features * width,
        4 * features * width,
        FULL,
        [
            pltpu.VMEM(pieces, bf16),
            pltpu.VMEM((pieces[0] // 4, *pieces[1:]), bf16),
            dma((4,)),
            dma((4,)),
        ],
    )(arrived)
    cross = lax.all_to_all(total, SAMP, 0, 0)

    def components(order, extra):
        n = len(order)
        first = not extra
        columns = 2 * n_l
        return call(
            lambda *refs: components_body(first, order, *refs),
            (
                jax.ShapeDtypeStruct((rows, n * depth), bf16),
                jax.ShapeDtypeStruct((rows, columns), f32),
            ),
            [SCALAR, SCALAR, whole(n_blocks, depth)]
            + [HBM] * (n + 1)
            + [whole(rows, 2 * n_l)] * len(extra),
            (whole(rows, n * depth), whole(rows, columns)),
            2 * rows * features * n * depth,
            2 * (rows * features + features * n * depth + rows * n * depth),
            FULL,
            [
                pltpu.VMEM((rows, features), bf16),
                pltpu.VMEM((features, n * depth), bf16),
                dma((n + 1,)),
            ],
        )(place, lambdas, squared, samples, *[blocks[b] for b in order], *extra)

    parts, state = [], ()
    for group in GROUPS:
        part, level = components(group, state)
        parts.append(part)
        state = (level,)

    order = sum(GROUPS, ()) + LAST
    return call(
        lambda *refs: fitted_body(len(GROUPS), order, *refs),
        jax.ShapeDtypeStruct((n_l, rows, width), f32),
        [SCALAR, SCALAR, whole(n_blocks, depth), whole(rows, 2 * n_l)]
        + [HBM] * (n_blocks + len(GROUPS) + 3),
        HBM,
        2 * n_l * rows * every * width,
        2 * rows * every + 2 * every * width + 4 * n_l * rows * width,
        FULL,
        [
            pltpu.VMEM((width + rows, features), bf16),
            pltpu.VMEM((rows, every), bf16),
            pltpu.VMEM((rows, width), bf16),
            pltpu.VMEM((features, every), bf16),
            pltpu.VMEM((width, every), bf16),
            pltpu.VMEM((n_l // 2, 2 * width, every), bf16),
            pltpu.VMEM((n_l, rows, width), f32),
            dma((n_blocks + len(GROUPS) + 4,)),
            dma((n_l,)),
        ],
    )(
        place, lambdas, squared, level, cross.reshape(2, width, -1), traits, samples,
        *parts,
        *[blocks[b] for b in order],
    )


def solution(mesh):
    split = Mesh(mesh.devices.reshape(8, 8, 4, 2), SAMP + TRAIT)
    return jax.shard_map(
        compute,
        mesh=split,
        in_specs=(P(SAMP, None), P(SAMP, TRAIT), P(None, TRAIT), P(), P()),
        out_specs=P(None, SAMP, TRAIT),
        check_vma=False,
    )
```
